512 devices in a mesh: section: 16 (over x, z_hi, core), tensor: 32 (over z_lo, y).
Axes of the slice: x: 4, y: 4, z: 16 (z_hi: 2, z_lo: 8; z = z_hi * 8 + z_lo), core: 2. Of those that a mesh axis runs over, the one named last changes fastest.
Arguments:
- context: bfloat16 [16, 256, 4096], P('section', None, 'tensor'), may hold values from -6 to 6
- out_weight: bfloat16 [16, 4096, 8192], P('section', 'tensor'), may hold values from -0.09375 to 0.09375
- residual: bfloat16 [16, 256, 8192], P('section', None, 'tensor'), may hold values from -36 to 36
- gain: float32 [16, 8192], P('section', 'tensor'), may hold values from 0.1 to 1.9
- q_weight: bfloat16 [16, 8192, 4096], P('section', None, 'tensor'), may hold values from -0.044194174 to 0.044194174
- kv_weight: bfloat16 [16, 8192, 1024], P('section', None, 'tensor'), may hold values from -0.044194174 to 0.044194174
Outputs:
- attended: bfloat16 [16, 256, 4096], P('section', None, 'tensor')
The draws below stay inside these ranges and needn't reach their ends.
All inputs are finite; a program needn't handle non-finite values.
Results may differ from the reference program's by a relative error of at most 0.033.
Values may be sent and summed in bfloat16 or wider, within the bound.
No kernel may reach another device: no remote copies, remote signals or barrier semaphores. Data moves between devices by JAX's collectives and lax.ppermute only.
A program may use at most 64 MiB of HBM per device.

```python
import jax
import jax.numpy as jnp
from jax import lax

D = 8192
HD = 128
GROUP = 8
SEQ = 256
HEADS = 32
KV_HEADS = 4
N_SECTION = 16
N_TENSOR = 32


def draw_residual(key, part):
    values = jnp.clip(jax.random.normal(key, (N_SECTION, SEQ, D), jnp.float32), -4.0, 4.0)
    position = jnp.arange(D).astype(jnp.float32) / D
    rising = 3.0 ** position
    return (values * rising[None, None, :]).astype(jnp.bfloat16)


def draw_q_weight(key, part):
    values = jnp.clip(jax.random.normal(key, (N_SECTION, D, HEADS * HD), jnp.float32), -4.0, 4.0)
    return (values * D ** (-0.5)).astype(jnp.bfloat16)


def draw_kv_weight(key, part):
    values = jnp.clip(jax.random.normal(key, (N_SECTION, D, 2 * HD * KV_HEADS), jnp.float32), -4.0, 4.0)
    return (values * D ** (-0.5)).astype(jnp.bfloat16)


def steps_of(stream_key, shape, split, smallest, top_value):
    def one(dim, blocks):
        heights = jax.random.uniform(jax.random.fold_in(jax.random.fold_in(stream_key, 6), dim), (blocks,), jnp.float32, smallest / len(split), top_value / len(split))
        return jnp.repeat(jnp.exp(heights), shape[dim] // blocks).reshape((-1,) + (1,) * (len(shape) - dim - 1))

    factor_of = one(*split[0])
    for cut in split[1:]:
        factor_of = factor_of * one(*cut)
    return factor_of


def gaussian(stream_key, extent, spread, most, shards=(), dtype=jnp.bfloat16):
    array = spread * jax.random.normal(stream_key, extent, jnp.float32)
    if shards:
        array = array * steps_of(stream_key, extent, shards, -0.22, 0.18)
    return jnp.clip(array, -most, most).astype(dtype)


def setup_inputs(seed: int = 0) -> dict:
    splits = jax.random.split(jax.random.key(seed), 7)
    context = gaussian(splits[0], (N_SECTION, SEQ, HEADS * HD), 1.0, 6.0, ((0, 16), (2, 32)))
    out_weight = gaussian(splits[1], (N_SECTION, HEADS * HD, D), (HEADS * HD) ** -0.5, 0.09375, ((0, 16), (1, 32)))
    residual = draw_residual(jax.random.fold_in(splits[6], 71), 0)
    gain = jnp.clip(1.0 + 0.18 * jax.random.normal(splits[3], (N_SECTION, D), jnp.float32), 0.1, 1.9)
    q_weight = draw_q_weight(jax.random.fold_in(splits[6], 71), 0)
    kv_weight = draw_kv_weight(jax.random.fold_in(splits[6], 71), 0)
    return dict(context=context, out_weight=out_weight, residual=residual, gain=gain, q_weight=q_weight, kv_weight=kv_weight)


THETA = 500000.0

def rotate(inputs, positions):
    half_width = inputs.shape[-1] // 2
    frequency = THETA ** (-(jnp.arange(half_width).astype(jnp.float32) * 2.0 / inputs.shape[-1]))
    angles = positions[:, None] * frequency[None, :]
    cosine = jnp.cos(angles)[:, None, :]
    sine_part = jnp.sin(angles)[:, None, :]
    first_half = inputs[..., :half_width]
    second_half = inputs[..., half_width:]
    return jnp.concatenate([first_half * cosine - second_half * sine_part, second_half * cosine + first_half * sine_part], axis=-1)

def reference(context, out_weight, residual, gain, q_weight, kv_weight):

    def send_section(inputs):
        local_context, local_out, local_residual = inputs

        def add_head(running, head_index):
            block_cols = lax.dynamic_slice_in_dim(local_context, head_index * HD, HD, 1)
            block_rows = lax.dynamic_slice_in_dim(local_out, head_index * HD, HD, 0)
            head_term = jnp.dot(block_cols, block_rows, preferred_element_type=jnp.float32).astype(jnp.bfloat16)
            head_term = lax.optimization_barrier(head_term)
            return (running + head_term.astype(jnp.float32), None)
        running, _ = lax.scan(add_head, jnp.zeros((SEQ, D), jnp.float32), jnp.arange(HEADS).astype(jnp.int32))
        return (local_residual.astype(jnp.float32) + running).astype(jnp.bfloat16)
    handover = lax.map(send_section, (context, out_weight, residual))
    received = jnp.roll(handover, 1, axis=0)
    positions = jnp.arange(SEQ).astype(jnp.float32)
    order = jnp.arange(SEQ)
    causal = order[:, None] >= order[None, :]
    feature_share = HD // N_TENSOR

    def receive(inputs):
        arriving, section_gain, query_cols, pair_cols = inputs
        values_f = arriving.astype(jnp.float32)
        normed = (values_f * lax.rsqrt(lax.optimization_barrier(jnp.mean(values_f * values_f, axis=-1, keepdims=True)) + 1e-05) * section_gain[None, :]).astype(jnp.bfloat16)
        queries = jnp.dot(normed, query_cols, preferred_element_type=jnp.float32).reshape(SEQ, HEADS, HD)
        queries = rotate(queries, positions).astype(jnp.bfloat16)
        pair_proj = jnp.dot(normed, pair_cols, preferred_element_type=jnp.float32).astype(jnp.bfloat16)
        pair_proj = pair_proj.reshape(SEQ, N_TENSOR, KV_HEADS, 2, feature_share)
        pair_proj = jnp.transpose(pair_proj, (0, 2, 3, 1, 4)).reshape(SEQ, KV_HEADS, 2, HD)
        keys = rotate(pair_proj[:, :, 0].astype(jnp.float32), positions).astype(jnp.bfloat16)
        values = pair_proj[:, :, 1]
        grouped = queries.reshape(SEQ, KV_HEADS, GROUP, HD).astype(jnp.float32)
        scores = jnp.einsum('sghd,tgd->ghst', grouped, keys.astype(jnp.float32)) * HD ** (-0.5)
        scores = jnp.where(causal[None, None], scores, -1e+30)
        softmax_weights = jax.nn.softmax(scores, axis=-1).astype(jnp.bfloat16)
        attended = jnp.einsum('ghst,tgd->sghd', softmax_weights.astype(jnp.float32), values.astype(jnp.float32))
        return attended.astype(jnp.bfloat16).reshape(SEQ, HEADS * HD)
    return lax.map(receive, (received, gain, q_weight, kv_weight))
```

```python
import jax
import jax.numpy as jnp
from jax import lax
from jax.sharding import Mesh, PartitionSpec as P

THETA = 500000.0
ROWS, COLS = 4, 8
BF16, F32 = jnp.bfloat16, jnp.float32


def contract(lhs, rhs, lhs_dim, rhs_dim):
    return lax.dot_general(
        lhs, rhs, (((lhs_dim,), (rhs_dim,)), ((), ())), preferred_element_type=F32
    )


def exchange(pieces, axis):
    return lax.all_to_all(pieces, axis, 0, 0, tiled=True)


def turn(rows, cosine, sine):
    half = rows.shape[0] // 2
    first, second = rows[:half], rows[half:]
    return jnp.concatenate(
        [first * cosine - second * sine, second * cosine + first * sine], axis=0
    )


def stats_rows(total):
    high = lax.reduce_precision(total, 8, 7)
    low = total - high
    rows = jnp.stack([high, low]).astype(BF16)
    return jnp.concatenate([rows, jnp.zeros((14, total.shape[0]), BF16)], axis=0)


def on_device(context, out_weight, residual, gain, q_weight, kv_weight):
    tokens, head = context.shape[1:]
    width = out_weight.shape[2]
    part = width // (ROWS * COLS)
    block = ROWS * part

    out_cols = out_weight[0].reshape(head, ROWS, COLS, part).transpose(2, 0, 1, 3)
    out_cols = out_cols.reshape(COLS, head, block)
    own = jnp.broadcast_to(context[0].T[None], (COLS, head, tokens))
    got = exchange(jnp.concatenate([out_cols, own], axis=2), "a")
    row_weight = got[:, :, :block].reshape(COLS * head, block)
    row_context = got[:, :, block:].reshape(COLS * head, tokens)
    terms = contract(row_weight, row_context, 0, 0).astype(BF16)

    q_rows = q_weight[0].reshape(ROWS, COLS, part, head).transpose(1, 0, 2, 3)
    q_block = exchange(q_rows.reshape(COLS, block, head), "a")
    kv_rows = kv_weight[0].T.reshape(ROWS, 8, width)
    kv_rows = exchange(kv_rows, "b")
    kv_rows = kv_rows.reshape(ROWS, 8, ROWS, COLS, part).transpose(3, 0, 1, 2, 4)
    kv_block = exchange(kv_rows.reshape(COLS, ROWS * 8, block), "a")
    kv_block = kv_block.reshape(COLS, ROWS, 2, 4, block).transpose(2, 1, 0, 3, 4)
    kv_block = kv_block.reshape(2 * head, block)

    terms = exchange(terms.reshape(ROWS, part, tokens), "b").astype(F32)
    handover = (residual[0].T.astype(F32) + jnp.sum(terms, axis=0)).astype(BF16)
    sections = lax.axis_size("section")
    received = lax.ppermute(
        handover, "section", [(i, (i + 1) % sections) for i in range(sections)]
    ).astype(F32)

    scaled = (received * gain[0][:, None]).astype(BF16)
    squares = stats_rows(jnp.sum(received * received, axis=0))
    gathered = lax.all_gather(jnp.concatenate([scaled, squares], axis=0), "b", axis=0)
    features = gathered[:, :part].reshape(block, tokens)
    squares = stats_rows(jnp.sum(gathered[:, part:part + 2].astype(F32), axis=(0, 1)))

    q_part = contract(q_block, features, 1, 0).astype(BF16)
    kv_part = contract(kv_block, features, 1, 0).astype(BF16)
    shared = jnp.concatenate([kv_part, squares], axis=0)
    shared = jnp.broadcast_to(shared[None], (COLS,) + shared.shape)
    summed = exchange(jnp.concatenate([q_part, shared], axis=1), "a").astype(F32)
    summed = jnp.sum(summed, axis=0)
    total = summed[3 * head] + summed[3 * head + 1]
    summed = summed[:3 * head] * lax.rsqrt(total / width + 1e-05)[None, :]

    positions = jnp.arange(tokens).astype(F32)
    frequency = THETA ** (-(jnp.arange(head // 2).astype(F32) * 2.0 / head))
    angles = frequency[:, None] * positions[None, :]
    cosine, sine = jnp.cos(angles), jnp.sin(angles)
    queries = turn(summed[:head], cosine, sine).astype(BF16)
    keys = summed[head:2 * head].astype(BF16).astype(F32)
    keys = turn(keys, cosine, sine).astype(BF16)
    values = summed[2 * head:].astype(BF16)
    scores = contract(queries, keys, 0, 0) * head ** (-0.5)
    order = jnp.arange(tokens)
    scores = jnp.where(order[:, None] >= order[None, :], scores, -1e30)
    softmax_weights = jax.nn.softmax(scores, axis=-1).astype(BF16)
    attended = contract(softmax_weights, values, 1, 1).astype(BF16)
    return attended[None]


def solution(mesh):
    sections = mesh.devices.shape[0]
    fine = Mesh(mesh.devices.reshape(sections, ROWS, COLS), ("section", "b", "a"))
    tensor = ("b", "a")
    placed = (
        P("section", None, tensor),
        P("section", tensor, None),
        P("section", None, tensor),
        P("section", tensor),
        P("section", None, tensor),
        P("section", None, tensor),
    )
    return jax.shard_map(
        on_device,
        mesh=fine,
        in_specs=placed,
        out_specs=P("section", None, tensor),
        check_vma=False,
    )
```

```python
import jax
import jax.numpy as jnp
from jax import lax
from jax.experimental import pallas as pl
from jax.experimental.pallas import tpu as pltpu
from jax.sharding import Mesh, PartitionSpec as P

THETA = 500000.0
ROWS, COLS = 4, 8
BF16, F32 = jnp.bfloat16, jnp.float32
VMEM = pl.BlockSpec(memory_space=pltpu.VMEM)
SMEM = pl.BlockSpec(memory_space=pltpu.SMEM)
STATS = 16


def contract(lhs, rhs, lhs_dim, rhs_dim):
    return lax.dot_general(
        lhs, rhs, (((lhs_dim,), (rhs_dim,)), ((), ())), preferred_element_type=F32
    )


def exchange(pieces, axis):
    return lax.all_to_all(pieces, axis, 0, 0, tiled=True)


def turn(rows, cosine, sine):
    half = rows.shape[0] // 2
    first, second = rows[:half], rows[half:]
    return jnp.concatenate(
        [first * cosine - second * sine, second * cosine + first * sine], axis=0
    )


def stats_rows(total):
    high = total.astype(BF16).astype(F32)
    index = lax.broadcasted_iota(jnp.int32, (STATS, total.shape[1]), 0)
    low = jnp.where(index == 1, total - high, 0.0)
    return jnp.where(index == 0, high, low).astype(BF16)


def call(body, name, outs, in_specs, *operands):
    return pl.pallas_call(
        body,
        in_specs=in_specs,
        out_specs=jax.tree.map(lambda _: VMEM, outs),
        out_shape=outs,
        compiler_params=pltpu.CompilerParams(vmem_limit_bytes=40 * 2**20),
        name=name,
    )(*operands)


def out_pieces(out_weight, context):
    head, width = out_weight.shape[1:]
    tokens = context.shape[1]
    part = width // (ROWS * COLS)

    def body(*refs):
        strips, own, out = refs[:ROWS], refs[ROWS], refs[ROWS + 1]
        for r in range(ROWS):
            out[0, :, r * part:(r + 1) * part] = strips[r][0]
        out[0, :, ROWS * part:] = own[0].astype(F32).T.astype(BF16)

    def strip(r):
        return pl.BlockSpec((1, head, part), lambda a: (0, 0, r * COLS + a))

    return pl.pallas_call(
        body,
        grid=(COLS,),
        in_specs=[strip(r) for r in range(ROWS)]
        + [pl.BlockSpec((1, tokens, head), lambda a: (0, 0, 0))],
        out_specs=pl.BlockSpec((1, head, ROWS * part + tokens), lambda a: (a, 0, 0)),
        out_shape=jax.ShapeDtypeStruct((COLS, head, ROWS * part + tokens), BF16),
        name="out_pieces",
    )(*[out_weight] * ROWS, context)


def in_pieces(q_weight, kv_weight):
    width, head = q_weight.shape[1:]
    cols = kv_weight.shape[0]
    part = width // (ROWS * COLS)
    block = ROWS * part
    rows = block + cols * block // head

    def body(*refs):
        q_refs, kv_refs, out = refs[:ROWS], refs[ROWS:2 * ROWS], refs[2 * ROWS]
        for r in range(ROWS):
            out[0, r * part:(r + 1) * part] = q_refs[r][0]
            for k in range(part // head):
                at = block + (r * (part // head) + k) * cols
                out[0, at:at + cols] = kv_refs[r][:, k * head:(k + 1) * head]

    def q_strip(r):
        return pl.BlockSpec((1, part, head), lambda a: (0, r * COLS + a, 0))

    def kv_strip(r):
        return pl.BlockSpec((cols, part), lambda a: (0, r * COLS + a))

    return pl.pallas_call(
        body,
        grid=(COLS,),
        in_specs=[q_strip(r) for r in range(ROWS)] + [kv_strip(r) for r in range(ROWS)],
        out_specs=pl.BlockSpec((1, rows, head), lambda a: (a, 0, 0)),
        out_shape=jax.ShapeDtypeStruct((COLS, rows, head), BF16),
        name="in_pieces",
    )(*[q_weight] * ROWS, *[kv_weight] * ROWS)


def row_terms(got, residual, row):
    head = got.shape[1]
    tokens, part = residual.shape[1:]

    def body(row_ref, got_ref, residual_ref, *outs):
        context = got_ref[:, :, ROWS * part:].reshape(COLS * head, tokens)
        for k in range(ROWS):
            at = pl.multiple_of((row_ref[0] ^ k) * part, part)
            weight = got_ref[:, :, pl.ds(at, part)].reshape(COLS * head, part)
            terms = contract(weight, context, 0, 0)
            if k == 0:
                terms = terms + residual_ref[0].astype(F32).T
            outs[k][...] = terms.astype(BF16)

    outs = [jax.ShapeDtypeStruct((part, tokens), BF16)] * ROWS
    return call(body, "row_terms", outs, [SMEM, VMEM, VMEM], row, got, residual)


def scaled_sum(pieces, gain):
    part, tokens = pieces[0].shape

    def body(*refs):
        total = refs[0][...].astype(F32)
        for k in range(1, ROWS):
            total = total + refs[k][...].astype(F32)
        out = refs[ROWS + 1]
        out[:part] = (total * refs[ROWS][...]).astype(BF16)
        out[part:] = stats_rows(jnp.sum(total * total, axis=0, keepdims=True))

    outs = jax.ShapeDtypeStruct((part + STATS, tokens), BF16)
    return call(body, "scaled_sum", outs, [VMEM] * (ROWS + 1), *pieces, gain)


def projections(got, gathered, row):
    rows, head = got.shape[1:]
    tokens = gathered.shape[2]
    part = gathered.shape[1] - STATS
    block = ROWS * part
    chunks = block // head
    cols = (rows - block) // chunks
    each = cols // ROWS
    half = each // 2

    def body(row_ref, got_ref, gathered_ref, q_ref, *refs):
        kv_refs, stats_ref, scratch = refs[:ROWS], refs[ROWS], refs[ROWS + 1]
        features = gathered_ref[:, :part].reshape(block, tokens)
        for a in range(COLS):
            q_ref[a] = contract(got_ref[a, :block], features, 0, 0).astype(BF16)
        kv = jnp.zeros((COLS * cols, tokens), F32)
        for k in range(chunks):
            at = block + k * cols
            weight = got_ref[:, at:at + cols].reshape(COLS * cols, head)
            kv = kv + contract(weight, features[k * head:(k + 1) * head], 1, 0)
        size = COLS * cols
        to = lax.broadcasted_iota(jnp.int32, (size, size), 0)
        source = lax.broadcasted_iota(jnp.int32, (size, size), 1)
        group, rest = to // (COLS * each), to % (COLS * each)
        kind, rest = rest // (COLS * half), rest % (COLS * half)
        column, feature = rest // half, rest % half
        wanted = column * cols + group * each + kind * half + feature
        select = jnp.where(source == wanted, 1.0, 0.0).astype(BF16)
        scratch[...] = contract(select, kv.astype(BF16), 1, 0).astype(BF16)
        for k in range(ROWS):
            at = pl.multiple_of((row_ref[0] ^ k) * COLS * each, COLS * each)
            kv_refs[k][...] = scratch[pl.ds(at, COLS * each)]
        squares = gathered_ref[:, part:].astype(F32)
        squares = jnp.sum(jnp.sum(squares, axis=0), axis=0, keepdims=True)
        stats_ref[...] = stats_rows(squares)

    shapes = [(COLS, head, tokens)] + [(COLS * each, tokens)] * ROWS + [(STATS, tokens)]
    return pl.pallas_call(
        body,
        in_specs=[SMEM, VMEM, VMEM],
        out_specs=[VMEM] * len(shapes),
        out_shape=[jax.ShapeDtypeStruct(shape, BF16) for shape in shapes],
        scratch_shapes=[pltpu.VMEM((COLS * cols, tokens), BF16)],
        compiler_params=pltpu.CompilerParams(vmem_limit_bytes=40 * 2**20),
        name="projections",
    )(row, got, gathered)


def head_pieces(q_part, kv_parts, stats, row):
    head, tokens = q_part.shape[1:]
    share = head // ROWS

    def body(row_ref, q_ref, *refs):
        kv_refs, stats_ref, out = refs[:ROWS], refs[ROWS], refs[ROWS + 1]
        for a in range(COLS):
            out[a, :head] = q_ref[a]
            out[a, 3 * head:] = stats_ref[...]
            for k in range(ROWS):
                at = pl.multiple_of((row_ref[0] ^ k) * share, share)
                out[a, pl.ds(head + at, share)] = kv_refs[k][:share]
                out[a, pl.ds(2 * head + at, share)] = kv_refs[k][share:]

    outs = jax.ShapeDtypeStruct((COLS, 3 * head + STATS, tokens), BF16)
    specs = [SMEM] + [VMEM] * (ROWS + 2)
    return call(body, "head_pieces", outs, specs, row, q_part, *kv_parts, stats)


def on_device(context, out_weight, residual, gain, q_weight, kv_weight):
    tokens, head = context.shape[1:]
    width = out_weight.shape[2]
    row = lax.axis_index("b").reshape(1)
    sections = lax.axis_size("section")

    def to_row(piece, step, distance):
        route = [
            (s * ROWS + r, (s + distance) % sections * ROWS + (r ^ step))
            for s in range(sections)
            for r in range(ROWS)
        ]
        return lax.ppermute(piece, ("section", "b"), route)

    got = exchange(out_pieces(out_weight, context), "a")
    terms = row_terms(got, residual, row)

    pieces = in_pieces(q_weight, kv_weight[0].T)
    pieces, *terms = lax.optimization_barrier((pieces, *terms))
    weights = exchange(pieces, "a")

    received = [to_row(terms[k], k, 1) for k in range(ROWS)]
    gathered = lax.all_gather(scaled_sum(received, gain.T), "b", axis=0)
    q_part, *kv_parts, stats = projections(weights, gathered, row)
    kv_parts = [kv_parts[0]] + [to_row(kv_parts[k], k, 0) for k in range(1, ROWS)]
    summed = exchange(head_pieces(q_part, kv_parts, stats, row), "a")
    summed = jnp.sum(summed.astype(F32), axis=0)
    total = summed[3 * head] + summed[3 * head + 1]
    summed = summed[:3 * head] * lax.rsqrt(total / width + 1e-05)[None, :]

    positions = jnp.arange(tokens).astype(F32)
    frequency = THETA ** (-(jnp.arange(head // 2).astype(F32) * 2.0 / head))
    angles = frequency[:, None] * positions[None, :]
    cosine, sine = jnp.cos(angles), jnp.sin(angles)
    queries = turn(summed[:head], cosine, sine).astype(BF16)
    keys = summed[head:2 * head].astype(BF16).astype(F32)
    keys = turn(keys, cosine, sine).astype(BF16)
    values = summed[2 * head:].astype(BF16)
    scores = contract(queries, keys, 0, 0) * head ** (-0.5)
    order = jnp.arange(tokens)
    scores = jnp.where(order[:, None] >= order[None, :], scores, -1e30)
    softmax_weights = jax.nn.softmax(scores, axis=-1).astype(BF16)
    attended = contract(softmax_weights, values, 1, 1).astype(BF16)
    return attended[None]


def solution(mesh):
    sections = mesh.devices.shape[0]
    fine = Mesh(mesh.devices.reshape(sections, ROWS, COLS), ("section", "b", "a"))
    tensor = ("b", "a")
    placed = (
        P("section", None, tensor),
        P("section", tensor, None),
        P("section", None, tensor),
        P("section", tensor),
        P("section", None, tensor),
        P("section", None, tensor),
    )
    return jax.shard_map(
        on_device,
        mesh=fine,
        in_specs=placed,
        out_specs=P("section", None, tensor),
        check_vma=False,
    )
```

```python
import jax
import jax.numpy as jnp
from jax import lax
from jax.experimental import pallas as pl
from jax.experimental.pallas import tpu as pltpu
from jax.sharding import Mesh, PartitionSpec as P

THETA = 500000.0
ROWS, PAIR, LINE = 4, 2, 4
COLS = PAIR * LINE
BF16, F32 = jnp.bfloat16, jnp.float32
VMEM = pl.BlockSpec(memory_space=pltpu.VMEM)
SMEM = pl.BlockSpec(memory_space=pltpu.SMEM)
STATS = 16


def contract(lhs, rhs, lhs_dim, rhs_dim):
    return lax.dot_general(
        lhs, rhs, (((lhs_dim,), (rhs_dim,)), ((), ())), preferred_element_type=F32
    )


def exchange(pieces, axis):
    return lax.all_to_all(pieces, axis, 0, 0, tiled=True)


def turn(rows, cosine, sine):
    half = rows.shape[0] // 2
    first, second = rows[:half], rows[half:]
    return jnp.concatenate(
        [first * cosine - second * sine, second * cosine + first * sine], axis=0
    )


def stats_rows(total):
    high = total.astype(BF16).astype(F32)
    index = lax.broadcasted_iota(jnp.int32, (STATS, total.shape[1]), 0)
    low = jnp.where(index == 1, total - high, 0.0)
    return jnp.where(index == 0, high, low).astype(BF16)


def call(body, name, outs, in_specs, *operands):
    return pl.pallas_call(
        body,
        in_specs=in_specs,
        out_specs=jax.tree.map(lambda _: VMEM, outs),
        out_shape=outs,
        compiler_params=pltpu.CompilerParams(vmem_limit_bytes=40 * 2**20),
        name=name,
    )(*operands)


def out_pieces(out_weight, context):
    head, width = out_weight.shape[1:]
    tokens = context.shape[1]
    part = width // (ROWS * COLS)
    block = ROWS * part

    def body(weight, own, out, staged, sems, out_sems):
        def strip(a, r):
            return pltpu.make_async_copy(
                weight.at[0, :, pl.ds((r * COLS + a) * part, part)],
                staged.at[a, :, pl.ds(r * part, part)],
                sems.at[a, r],
            )

        for a in range(COLS):
            for r in range(ROWS):
                strip(a, r).start()
        turned = own[0].astype(F32).T.astype(BF16)
        for a in range(COLS):
            staged[a, :, block:] = turned
        outs = [pltpu.make_async_copy(staged.at[a], out.at[a], out_sems.at[a]) for a in range(COLS)]
        for a in range(COLS):
            for r in range(ROWS):
                strip(a, r).wait()
            outs[a].start()
        for copy in outs:
            copy.wait()

    shape = (COLS, head, block + tokens)
    return pl.pallas_call(
        body,
        in_specs=[pl.BlockSpec(memory_space=pl.ANY), VMEM],
        out_specs=pl.BlockSpec(memory_space=pl.ANY),
        out_shape=jax.ShapeDtypeStruct(shape, BF16),
        scratch_shapes=[
            pltpu.VMEM(shape, BF16),
            pltpu.SemaphoreType.DMA((COLS, ROWS)),
            pltpu.SemaphoreType.DMA((COLS,)),
        ],
        compiler_params=pltpu.CompilerParams(vmem_limit_bytes=40 * 2**20),
        name="out_pieces",
    )(out_weight, context)


def in_pieces(q_weight, kv_weight, side):
    width, head = q_weight.shape[1:]
    cols = kv_weight.shape[0]
    part = width // (ROWS * COLS)
    strips = ROWS * PAIR
    block = strips * part
    rows = block + cols * block // head

    def body(side_ref, *refs):
        q_refs, kv_refs, out = refs[:strips], refs[strips:2 * strips], refs[2 * strips]
        for r in range(strips):
            out[0, r * part:(r + 1) * part] = q_refs[r][0]
            for k in range(part // head):
                at = block + (r * (part // head) + k) * cols
                out[0, at:at + cols] = kv_refs[r][:, k * head:(k + 1) * head]

    def place(r, y, side_ref):
        return r % ROWS * COLS + (side_ref[0] ^ (r // ROWS)) * LINE + y

    def q_strip(r):
        return pl.BlockSpec((1, part, head), lambda y, s: (0, place(r, y, s), 0))

    def kv_strip(r):
        return pl.BlockSpec((cols, part), lambda y, s: (0, place(r, y, s)))

    return pl.pallas_call(
        body,
        grid_spec=pltpu.PrefetchScalarGridSpec(
            num_scalar_prefetch=1,
            grid=(LINE,),
            in_specs=[q_strip(r) for r in range(strips)]
            + [kv_strip(r) for r in range(strips)],
            out_specs=pl.BlockSpec((1, rows, head), lambda y, s: (y, 0, 0)),
        ),
        out_shape=jax.ShapeDtypeStruct((LINE, rows, head), BF16),
        name="in_pieces",
    )(side, *[q_weight] * strips, *[kv_weight] * strips)


def row_terms(got, residual, row):
    head = got.shape[1]
    tokens, part = residual.shape[1:]

    def body(row_ref, got_ref, residual_ref, *outs):
        context = got_ref[:, :, ROWS * part:].reshape(COLS * head, tokens)
        for k in range(ROWS):
            at = pl.multiple_of((row_ref[0] ^ k) * part, part)
            weight = got_ref[:, :, pl.ds(at, part)].reshape(COLS * head, part)
            terms = contract(weight, context, 0, 0)
            if k == 0:
                terms = terms + residual_ref[0].astype(F32).T
            outs[k][...] = terms.astype(BF16)

    outs = [jax.ShapeDtypeStruct((part, tokens), BF16)] * ROWS
    return call(body, "row_terms", outs, [SMEM, VMEM, VMEM], row, got, residual)


def scaled_sum(pieces, gain):
    part, tokens = pieces[0].shape

    def body(*refs):
        total = refs[0][...].astype(F32)
        for k in range(1, ROWS):
            total = total + refs[k][...].astype(F32)
        out = refs[ROWS + 1]
        out[:part] = (total * refs[ROWS][...]).astype(BF16)
        out[part:] = stats_rows(jnp.sum(total * total, axis=0, keepdims=True))

    outs = jax.ShapeDtypeStruct((part + STATS, tokens), BF16)
    return call(body, "scaled_sum", outs, [VMEM] * (ROWS + 1), *pieces, gain)


def projections(got, own, other):
    rows, head = got.shape[1:]
    tokens = own.shape[2]
    part = own.shape[1] - STATS
    half = ROWS * part
    block = PAIR * half
    chunks = block // head
    cols = (rows - block) // chunks
    each = cols // ROWS
    size = LINE * cols

    def body(got_ref, own_ref, other_ref, out):
        sides = [ref[:, :part].reshape(half, tokens) for ref in (own_ref, other_ref)]
        features = jnp.concatenate(sides, axis=0)
        kv = jnp.zeros((size, tokens), F32)
        for k in range(chunks):
            at = block + k * cols
            weight = got_ref[:, at:at + cols].reshape(size, head)
            kv = kv + contract(weight, features[k * head:(k + 1) * head], 1, 0)
        to = lax.broadcasted_iota(jnp.int32, (size, size), 0)
        source = lax.broadcasted_iota(jnp.int32, (size, size), 1)
        group, rest = to // (LINE * each), to % (LINE * each)
        kind, rest = rest // (LINE * each // 2), rest % (LINE * each // 2)
        column, feature = rest // (each // 2), rest % (each // 2)
        wanted = column * cols + group * each + kind * (each // 2) + feature
        select = jnp.where(source == wanted, 1.0, 0.0).astype(BF16)
        kv = contract(select, kv.astype(BF16), 1, 0).astype(BF16)
        squares = own_ref[:, part:].astype(F32) + other_ref[:, part:].astype(F32)
        squares = jnp.sum(jnp.sum(squares, axis=0), axis=0, keepdims=True)
        stats = stats_rows(squares)
        for y in range(LINE):
            out[y, :head] = contract(got_ref[y, :block], features, 0, 0).astype(BF16)
            out[y, head:head + size] = kv
            out[y, head + size:] = stats

    outs = jax.ShapeDtypeStruct((LINE, head + size + STATS, tokens), BF16)
    return call(body, "projections", outs, [VMEM] * 3, got, own, other)


def head_inputs(got, cosine, sine, width):
    line, rows, tokens = got.shape
    head = 2 * cosine.shape[0]
    share = (rows - head - STATS) // ROWS

    def body(got_ref, cosine_ref, sine_ref, q_ref, kv_ref):
        total = got_ref[0].astype(F32)
        for y in range(1, line):
            total = total + got_ref[y].astype(F32)
        squares = jnp.sum(total[rows - STATS:], axis=0, keepdims=True)
        total = total[:rows - STATS] * lax.rsqrt(squares / width + 1e-05)
        q_ref[...] = turn(total[:head], cosine_ref[...], sine_ref[...]).astype(BF16)
        for r in range(ROWS):
            at = head + r * share
            for z in range(PAIR):
                kv_ref[r * PAIR + z] = total[at:at + share].astype(BF16)

    outs = [
        jax.ShapeDtypeStruct((head, tokens), BF16),
        jax.ShapeDtypeStruct((ROWS * PAIR, share, tokens), BF16),
    ]
    return call(body, "head_inputs", outs, [VMEM] * 3, got, cosine, sine)


def attention(queries, pairs, cosine, sine):
    head, tokens = queries.shape
    groups, share = pairs.shape[:2]

    def body(q_ref, pairs_ref, cosine_ref, sine_ref, out):
        keys = pairs_ref[:, :share // 2].reshape(head, tokens).astype(F32)
        values = pairs_ref[:, share // 2:].reshape(head, tokens)
        keys = turn(keys, cosine_ref[...], sine_ref[...]).astype(BF16)
        scores = contract(q_ref[...], keys, 0, 0) * head ** (-0.5)
        at = lax.broadcasted_iota(jnp.int32, (tokens, tokens), 0)
        key_at = lax.broadcasted_iota(jnp.int32, (tokens, tokens), 1)
        scores = jnp.where(at >= key_at, scores, -1e30)
        weights = jnp.exp(scores - jnp.max(scores, axis=1, keepdims=True))
        weights = weights / jnp.sum(weights, axis=1, keepdims=True)
        out[0] = contract(weights.astype(BF16), values, 1, 1).astype(BF16)

    outs = jax.ShapeDtypeStruct((1, tokens, head), BF16)
    return call(body, "attention", outs, [VMEM] * 4, queries, pairs, cosine, sine)


def on_device(context, out_weight, residual, gain, q_weight, kv_weight):
    tokens, head = context.shape[1:]
    width = out_weight.shape[2]
    row = lax.axis_index("b").reshape(1)
    sections = lax.axis_size("section")

    def to_row(piece, step, distance):
        route = [
            (s * ROWS + r, (s + distance) % sections * ROWS + (r ^ step))
            for s in range(sections)
            for r in range(ROWS)
        ]
        return lax.ppermute(piece, ("section", "b"), route)

    got = exchange(out_pieces(out_weight, context), ("z", "y"))
    terms = row_terms(got, residual, row)

    pieces = in_pieces(q_weight, kv_weight[0].T, lax.axis_index("z").reshape(1))
    pieces, *terms = lax.optimization_barrier((pieces, *terms))
    weights = exchange(pieces, "y")

    positions = jnp.arange(tokens).astype(F32)
    frequency = THETA ** (-(jnp.arange(head // 2).astype(F32) * 2.0 / head))
    angles = frequency[:, None] * positions[None, :]
    cosine, sine = jnp.cos(angles), jnp.sin(angles)

    received = [to_row(terms[k], k, 1) for k in range(ROWS)]
    gathered = lax.all_gather(scaled_sum(received, gain.T), "b", axis=0)
    other = lax.ppermute(gathered, "z", [(0, 1), (1, 0)])
    summed = exchange(projections(weights, gathered, other), "y")
    queries, pairs = head_inputs(summed, cosine, sine, width)
    return attention(queries, exchange(pairs, ("b", "z")), cosine, sine)


def solution(mesh):
    sections = mesh.devices.shape[0]
    fine = Mesh(mesh.devices.reshape(sections, ROWS, PAIR, LINE), ("section", "b", "z", "y"))
    tensor = ("b", "z", "y")
    placed = (
        P("section", None, tensor),
        P("section", tensor, None),
        P("section", None, tensor),
        P("section", tensor),
        P("section", None, tensor),
        P("section", None, tensor),
    )
    return jax.shard_map(
        on_device,
        mesh=fine,
        in_specs=placed,
        out_specs=P("section", None, tensor),
        check_vma=False,
    )
```

```python
import jax
import jax.numpy as jnp
from jax import lax
from jax.experimental import pallas as pl
from jax.experimental.pallas import tpu as pltpu
from jax.sharding import Mesh, PartitionSpec as P

THETA = 500000.0
ROWS, PAIR, LINE = 4, 2, 4
COLS = PAIR * LINE
BF16, F32 = jnp.bfloat16, jnp.float32
VMEM = pl.BlockSpec(memory_space=pltpu.VMEM)
SMEM = pl.BlockSpec(memory_space=pltpu.SMEM)
STATS = 16


def contract(lhs, rhs, lhs_dim, rhs_dim):
    return lax.dot_general(
        lhs, rhs, (((lhs_dim,), (rhs_dim,)), ((), ())), preferred_element_type=F32
    )


def exchange(pieces, axis):
    return lax.all_to_all(pieces, axis, 0, 0, tiled=True)


def turn(rows, cosine, sine):
    half = rows.shape[0] // 2
    first, second = rows[:half], rows[half:]
    return jnp.concatenate(
        [first * cosine - second * sine, second * cosine + first * sine], axis=0
    )


def stats_rows(total):
    high = total.astype(BF16).astype(F32)
    index = lax.broadcasted_iota(jnp.int32, (STATS, total.shape[1]), 0)
    low = jnp.where(index == 1, total - high, 0.0)
    return jnp.where(index == 0, high, low).astype(BF16)


def call(body, name, outs, in_specs, *operands):
    return pl.pallas_call(
        body,
        in_specs=in_specs,
        out_specs=jax.tree.map(lambda _: VMEM, outs),
        out_shape=outs,
        compiler_params=pltpu.CompilerParams(vmem_limit_bytes=40 * 2**20),
        name=name,
    )(*operands)


def out_pieces(out_weight, context):
    head, width = out_weight.shape[1:]
    tokens = context.shape[1]
    part = width // (ROWS * COLS)
    block = ROWS * part

    def body(weight, own, out, staged, sems, out_sems):
        def strip(a, r):
            return pltpu.make_async_copy(
                weight.at[0, :, pl.ds((r * COLS + a) * part, part)],
                staged.at[a, :, pl.ds(r * part, part)],
                sems.at[a, r],
            )

        for a in range(COLS):
            for r in range(ROWS):
                strip(a, r).start()
        turned = own[0].astype(F32).T.astype(BF16)
        for a in range(COLS):
            staged[a, :, block:] = turned
        outs = [pltpu.make_async_copy(staged.at[a], out.at[a], out_sems.at[a]) for a in range(COLS)]
        for a in range(COLS):
            for r in range(ROWS):
                strip(a, r).wait()
            outs[a].start()
        for copy in outs:
            copy.wait()

    shape = (COLS, head, block + tokens)
    return pl.pallas_call(
        body,
        in_specs=[pl.BlockSpec(memory_space=pl.ANY), VMEM],
        out_specs=pl.BlockSpec(memory_space=pl.ANY),
        out_shape=jax.ShapeDtypeStruct(shape, BF16),
        scratch_shapes=[
            pltpu.VMEM(shape, BF16),
            pltpu.SemaphoreType.DMA((COLS, ROWS)),
            pltpu.SemaphoreType.DMA((COLS,)),
        ],
        compiler_params=pltpu.CompilerParams(vmem_limit_bytes=40 * 2**20),
        name="out_pieces",
    )(out_weight, context)


def in_pieces(q_weight, kv_weight, side):
    width, head = q_weight.shape[1:]
    cols = kv_weight.shape[0]
    part = width // (ROWS * COLS)
    strips = ROWS * PAIR
    block = strips * part
    rows = block + cols * block // head

    def body(side_ref, *refs):
        q_refs, kv_refs, out = refs[:strips], refs[strips:2 * strips], refs[2 * strips]
        for r in range(strips):
            out[0, r * part:(r + 1) * part] = q_refs[r][0]
            for k in range(part // head):
                at = block + (r * (part // head) + k) * cols
                out[0, at:at + cols] = kv_refs[r][:, k * head:(k + 1) * head]

    def place(r, y, side_ref):
        return r % ROWS * COLS + (side_ref[0] ^ (r // ROWS)) * LINE + (side_ref[1] ^ y)

    def q_strip(r):
        return pl.BlockSpec((1, part, head), lambda y, s: (0, place(r, y, s), 0))

    def kv_strip(r):
        return pl.BlockSpec((cols, part), lambda y, s: (0, place(r, y, s)))

    return pl.pallas_call(
        body,
        grid_spec=pltpu.PrefetchScalarGridSpec(
            num_scalar_prefetch=1,
            grid=(LINE,),
            in_specs=[q_strip(r) for r in range(strips)]
            + [kv_strip(r) for r in range(strips)],
            out_specs=pl.BlockSpec((1, rows, head), lambda y, s: (y, 0, 0)),
        ),
        out_shape=jax.ShapeDtypeStruct((LINE, rows, head), BF16),
        name="in_pieces",
    )(side, *[q_weight] * strips, *[kv_weight] * strips)


def row_terms(got, residual, row):
    head = got.shape[1]
    tokens, part = residual.shape[1:]

    def body(row_ref, got_ref, residual_ref, *outs):
        context = got_ref[:, :, ROWS * part:].reshape(COLS * head, tokens)
        for k in range(ROWS):
            at = pl.multiple_of((row_ref[0] ^ k) * part, part)
            weight = got_ref[:, :, pl.ds(at, part)].reshape(COLS * head, part)
            terms = contract(weight, context, 0, 0)
            if k == 0:
                terms = terms + residual_ref[0].astype(F32).T
            outs[k][...] = terms.astype(BF16)

    outs = [jax.ShapeDtypeStruct((part, tokens), BF16)] * ROWS
    return call(body, "row_terms", outs, [SMEM, VMEM, VMEM], row, got, residual)


def scaled_sum(pieces, gain):
    part, tokens = pieces[0].shape

    def body(*refs):
        total = refs[0][...].astype(F32)
        for k in range(1, ROWS):
            total = total + refs[k][...].astype(F32)
        out = refs[ROWS + 1]
        out[:part] = (total * refs[ROWS][...]).astype(BF16)
        out[part:] = stats_rows(jnp.sum(total * total, axis=0, keepdims=True))

    outs = jax.ShapeDtypeStruct((part + STATS, tokens), BF16)
    return call(body, "scaled_sum", outs, [VMEM] * (ROWS + 1), *pieces, gain)


def projections(got, own, other, line):
    rows, head = got[0].shape
    tokens = own.shape[2]
    part = own.shape[1] - STATS
    half = ROWS * part
    block = PAIR * half
    chunks = block // head
    cols = (rows - block) // chunks
    each = cols // ROWS
    size = LINE * cols

    def body(line_ref, *refs):
        got_refs, (own_ref, other_ref, out) = refs[:LINE], refs[LINE:]
        sides = [ref[:, :part].reshape(half, tokens) for ref in (own_ref, other_ref)]
        features = jnp.concatenate(sides, axis=0)
        kv = jnp.zeros((size, tokens), F32)
        for k in range(chunks):
            at = block + k * cols
            weight = jnp.concatenate([ref[at:at + cols] for ref in got_refs], axis=0)
            kv = kv + contract(weight, features[k * head:(k + 1) * head], 1, 0)
        to = lax.broadcasted_iota(jnp.int32, (size, size), 0)
        source = lax.broadcasted_iota(jnp.int32, (size, size), 1)
        group, rest = to // (LINE * each), to % (LINE * each)
        kind, rest = rest // (LINE * each // 2), rest % (LINE * each // 2)
        column, feature = rest // (each // 2), rest % (each // 2)
        wanted = (column ^ line_ref[0]) * cols + group * each + kind * (each // 2) + feature
        select = jnp.where(source == wanted, 1.0, 0.0).astype(BF16)
        kv = contract(select, kv.astype(BF16), 1, 0).astype(BF16)
        squares = own_ref[:, part:].astype(F32) + other_ref[:, part:].astype(F32)
        squares = jnp.sum(jnp.sum(squares, axis=0), axis=0, keepdims=True)
        stats = stats_rows(squares)
        for y in range(LINE):
            out[line_ref[0] ^ y, :head] = contract(got_refs[y][:block], features, 0, 0).astype(BF16)
            out[y, head:head + size] = kv
            out[y, head + size:] = stats

    outs = jax.ShapeDtypeStruct((LINE, head + size + STATS, tokens), BF16)
    specs = [SMEM] + [VMEM] * (LINE + 2)
    return call(body, "projections", outs, specs, line, *got, own, other)


def head_inputs(got, cosine, sine, width):
    line, rows, tokens = got.shape
    head = 2 * cosine.shape[0]
    share = (rows - head - STATS) // ROWS

    def body(got_ref, cosine_ref, sine_ref, q_ref, kv_ref):
        total = got_ref[0].astype(F32)
        for y in range(1, line):
            total = total + got_ref[y].astype(F32)
        squares = jnp.sum(total[rows - STATS:], axis=0, keepdims=True)
        total = total[:rows - STATS] * lax.rsqrt(squares / width + 1e-05)
        q_ref[...] = turn(total[:head], cosine_ref[...], sine_ref[...]).astype(BF16)
        for r in range(ROWS):
            at = head + r * share
            for z in range(PAIR):
                kv_ref[r * PAIR + z] = total[at:at + share].astype(BF16)

    outs = [
        jax.ShapeDtypeStruct((head, tokens), BF16),
        jax.ShapeDtypeStruct((ROWS * PAIR, share, tokens), BF16),
    ]
    return call(body, "head_inputs", outs, [VMEM] * 3, got, cosine, sine)


def attention(queries, pairs, cosine, sine):
    head, tokens = queries.shape
    groups, share = pairs.shape[:2]

    def body(q_ref, pairs_ref, cosine_ref, sine_ref, out):
        keys = pairs_ref[:, :share // 2].reshape(head, tokens).astype(F32)
        values = pairs_ref[:, share // 2:].reshape(head, tokens)
        keys = turn(keys, cosine_ref[...], sine_ref[...]).astype(BF16)
        scores = contract(q_ref[...], keys, 0, 0) * head ** (-0.5)
        at = lax.broadcasted_iota(jnp.int32, (tokens, tokens), 0)
        key_at = lax.broadcasted_iota(jnp.int32, (tokens, tokens), 1)
        scores = jnp.where(at >= key_at, scores, -1e30)
        weights = jnp.exp(scores - jnp.max(scores, axis=1, keepdims=True))
        weights = weights / jnp.sum(weights, axis=1, keepdims=True)
        out[0] = contract(weights.astype(BF16), values, 1, 1).astype(BF16)

    outs = jax.ShapeDtypeStruct((1, tokens, head), BF16)
    return call(body, "attention", outs, [VMEM] * 4, queries, pairs, cosine, sine)


def on_device(context, out_weight, residual, gain, q_weight, kv_weight):
    tokens, head = context.shape[1:]
    width = out_weight.shape[2]
    row = lax.axis_index("b").reshape(1)
    line = lax.axis_index("y").reshape(1)
    sections = lax.axis_size("section")

    def to_row(piece, step, distance):
        route = [
            (s * ROWS + r, (s + distance) % sections * ROWS + (r ^ step))
            for s in range(sections)
            for r in range(ROWS)
        ]
        return lax.ppermute(piece, ("section", "b"), route)

    got = exchange(out_pieces(out_weight, context), ("z", "y"))
    terms = row_terms(got, residual, row)

    pieces = in_pieces(q_weight, kv_weight[0].T, jnp.stack([lax.axis_index("z"), line[0]]))
    weights = [pieces[0]]
    for k in range(1, LINE):
        weights.append(lax.ppermute(pieces[k], "y", [(y, y ^ k) for y in range(LINE)]))

    positions = jnp.arange(tokens).astype(F32)
    frequency = THETA ** (-(jnp.arange(head // 2).astype(F32) * 2.0 / head))
    angles = frequency[:, None] * positions[None, :]
    cosine, sine = jnp.cos(angles), jnp.sin(angles)

    received = [to_row(terms[k], k, 1) for k in range(ROWS)]
    gathered = lax.all_gather(scaled_sum(received, gain.T), "b", axis=0)
    other = lax.ppermute(gathered, "z", [(0, 1), (1, 0)])
    summed = exchange(projections(weights, gathered, other, line), "y")
    queries, pairs = head_inputs(summed, cosine, sine, width)
    return attention(queries, exchange(pairs, ("b", "z")), cosine, sine)


def solution(mesh):
    sections = mesh.devices.shape[0]
    fine = Mesh(mesh.devices.reshape(sections, ROWS, PAIR, LINE), ("section", "b", "z", "y"))
    tensor = ("b", "z", "y")
    placed = (
        P("section", None, tensor),
        P("section", tensor, None),
        P("section", None, tensor),
        P("section", tensor),
        P("section", None, tensor),
        P("section", None, tensor),
    )
    return jax.shard_map(
        on_device,
        mesh=fine,
        in_specs=placed,
        out_specs=P("section", None, tensor),
        check_vma=False,
    )
```

```python
import jax
import jax.numpy as jnp
from jax import lax
from jax.experimental import pallas as pl
from jax.experimental.pallas import tpu as pltpu
from jax.sharding import Mesh, PartitionSpec as P

THETA = 500000.0
ROWS, PAIR, LINE = 4, 2, 4
COLS = PAIR * LINE
BF16, F32 = jnp.bfloat16, jnp.float32
VMEM = pl.BlockSpec(memory_space=pltpu.VMEM)
SMEM = pl.BlockSpec(memory_space=pltpu.SMEM)
STATS = 16


def contract(lhs, rhs, lhs_dim, rhs_dim):
    return lax.dot_general(
        lhs, rhs, (((lhs_dim,), (rhs_dim,)), ((), ())), preferred_element_type=F32
    )


def exchange(pieces, axis):
    return lax.all_to_all(pieces, axis, 0, 0, tiled=True)


def turn(rows, cosine, sine):
    half = rows.shape[0] // 2
    first, second = rows[:half], rows[half:]
    return jnp.concatenate(
        [first * cosine - second * sine, second * cosine + first * sine], axis=0
    )


def stats_rows(total):
    high = total.astype(BF16).astype(F32)
    index = lax.broadcasted_iota(jnp.int32, (STATS, total.shape[1]), 0)
    low = jnp.where(index == 1, total - high, 0.0)
    return jnp.where(index == 0, high, low).astype(BF16)


def call(body, name, outs, in_specs, *operands):
    return pl.pallas_call(
        body,
        in_specs=in_specs,
        out_specs=jax.tree.map(lambda _: VMEM, outs),
        out_shape=outs,
        compiler_params=pltpu.CompilerParams(vmem_limit_bytes=40 * 2**20),
        name=name,
    )(*operands)


def out_pieces(out_weight, context):
    head, width = out_weight.shape[1:]
    tokens = context.shape[1]
    part = width // (ROWS * COLS)
    block = ROWS * part

    def body(weight, own, out):
        for r in range(ROWS):
            at = pl.multiple_of((r * COLS + pl.program_id(0)) * part, part)
            out[0, :, r * part:(r + 1) * part] = weight[0, :, pl.ds(at, part)]
        out[0, :, block:] = own[0].astype(F32).T.astype(BF16)

    return pl.pallas_call(
        body,
        grid=(COLS,),
        in_specs=[VMEM, VMEM],
        out_specs=pl.BlockSpec((1, head, block + tokens), lambda a: (a, 0, 0)),
        out_shape=jax.ShapeDtypeStruct((COLS, head, block + tokens), BF16),
        compiler_params=pltpu.CompilerParams(vmem_limit_bytes=40 * 2**20),
        name="out_pieces",
    )(out_weight, context)


def in_pieces(q_weight, kv_weight, side):
    width, head = q_weight.shape[1:]
    cols = kv_weight.shape[0]
    part = width // (ROWS * COLS)
    strips = ROWS * PAIR
    block = strips * part
    rows = block + cols * block // head

    def body(side_ref, *refs):
        q_refs, kv_refs, out = refs[:strips], refs[strips:2 * strips], refs[2 * strips]
        for r in range(strips):
            out[0, r * part:(r + 1) * part] = q_refs[r][0]
            for k in range(part // head):
                at = block + (r * (part // head) + k) * cols
                out[0, at:at + cols] = kv_refs[r][:, k * head:(k + 1) * head]

    def place(r, y, side_ref):
        return r % ROWS * COLS + (side_ref[0] ^ (r // ROWS)) * LINE + (side_ref[1] ^ y)

    def q_strip(r):
        return pl.BlockSpec((1, part, head), lambda y, s: (0, place(r, y, s), 0))

    def kv_strip(r):
        return pl.BlockSpec((cols, part), lambda y, s: (0, place(r, y, s)))

    return pl.pallas_call(
        body,
        grid_spec=pltpu.PrefetchScalarGridSpec(
            num_scalar_prefetch=1,
            grid=(LINE,),
            in_specs=[q_strip(r) for r in range(strips)]
            + [kv_strip(r) for r in range(strips)],
            out_specs=pl.BlockSpec((1, rows, head), lambda y, s: (y, 0, 0)),
        ),
        out_shape=jax.ShapeDtypeStruct((LINE, rows, head), BF16),
        name="in_pieces",
    )(side, *[q_weight] * strips, *[kv_weight] * strips)


def row_terms(got, residual, row):
    head = got.shape[1]
    tokens, part = residual.shape[1:]

    def body(row_ref, got_ref, residual_ref, *outs):
        context = got_ref[:, :, ROWS * part:].reshape(COLS * head, tokens)
        for k in range(ROWS):
            at = pl.multiple_of((row_ref[0] ^ k) * part, part)
            weight = got_ref[:, :, pl.ds(at, part)].reshape(COLS * head, part)
            terms = contract(weight, context, 0, 0)
            if k == 0:
                terms = terms + residual_ref[0].astype(F32).T
            outs[k][...] = terms.astype(BF16)

    outs = [jax.ShapeDtypeStruct((part, tokens), BF16)] * ROWS
    return call(body, "row_terms", outs, [SMEM, VMEM, VMEM], row, got, residual)


def scaled_sum(pieces, gain):
    part, tokens = pieces[0].shape

    def body(*refs):
        total = refs[0][...].astype(F32)
        for k in range(1, ROWS):
            total = total + refs[k][...].astype(F32)
        out = refs[ROWS + 1]
        out[:part] = (total * refs[ROWS][...]).astype(BF16)
        out[part:] = stats_rows(jnp.sum(total * total, axis=0, keepdims=True))

    outs = jax.ShapeDtypeStruct((part + STATS, tokens), BF16)
    return call(body, "scaled_sum", outs, [VMEM] * (ROWS + 1), *pieces, gain)


def projections(got, own, other, line):
    rows, head = got[0].shape
    tokens = own.shape[2]
    part = own.shape[1] - STATS
    half = ROWS * part
    block = PAIR * half
    chunks = block // head
    cols = (rows - block) // chunks
    each = cols // ROWS
    size = LINE * cols

    def body(line_ref, *refs):
        got_refs, (own_ref, other_ref, out) = refs[:LINE], refs[LINE:]
        sides = [ref[:, :part].reshape(half, tokens) for ref in (own_ref, other_ref)]
        features = jnp.concatenate(sides, axis=0)
        kv = jnp.zeros((size, tokens), F32)
        for k in range(chunks):
            at = block + k * cols
            weight = jnp.concatenate([ref[at:at + cols] for ref in got_refs], axis=0)
            kv = kv + contract(weight, features[k * head:(k + 1) * head], 1, 0)
        to = lax.broadcasted_iota(jnp.int32, (size, size), 0)
        source = lax.broadcasted_iota(jnp.int32, (size, size), 1)
        group, rest = to // (LINE * each), to % (LINE * each)
        kind, rest = rest // (LINE * each // 2), rest % (LINE * each // 2)
        column, feature = rest // (each // 2), rest % (each // 2)
        wanted = (column ^ line_ref[0]) * cols + group * each + kind * (each // 2) + feature
        select = jnp.where(source == wanted, 1.0, 0.0).astype(BF16)
        kv = contract(select, kv.astype(BF16), 1, 0).astype(BF16)
        squares = own_ref[:, part:].astype(F32) + other_ref[:, part:].astype(F32)
        squares = jnp.sum(jnp.sum(squares, axis=0), axis=0, keepdims=True)
        stats = stats_rows(squares)
        for y in range(LINE):
            out[line_ref[0] ^ y, :head] = contract(got_refs[y][:block], features, 0, 0).astype(BF16)
            out[y, head:head + size] = kv
            out[y, head + size:] = stats

    outs = jax.ShapeDtypeStruct((LINE, head + size + STATS, tokens), BF16)
    specs = [SMEM] + [VMEM] * (LINE + 2)
    return call(body, "projections", outs, specs, line, *got, own, other)


def head_inputs(got, cosine, sine, width):
    line, rows, tokens = got.shape
    head = 2 * cosine.shape[0]
    share = (rows - head - STATS) // ROWS

    def body(got_ref, cosine_ref, sine_ref, q_ref, kv_ref):
        total = got_ref[0].astype(F32)
        for y in range(1, line):
            total = total + got_ref[y].astype(F32)
        squares = jnp.sum(total[rows - STATS:], axis=0, keepdims=True)
        total = total[:rows - STATS] * lax.rsqrt(squares / width + 1e-05)
        q_ref[...] = turn(total[:head], cosine_ref[...], sine_ref[...]).astype(BF16)
        for r in range(ROWS):
            at = head + r * share
            for z in range(PAIR):
                kv_ref[r * PAIR + z] = total[at:at + share].astype(BF16)

    outs = [
        jax.ShapeDtypeStruct((head, tokens), BF16),
        jax.ShapeDtypeStruct((ROWS * PAIR, share, tokens), BF16),
    ]
    return call(body, "head_inputs", outs, [VMEM] * 3, got, cosine, sine)


def attention(queries, pairs, cosine, sine):
    head, tokens = queries.shape
    groups, share = pairs.shape[:2]

    def body(q_ref, pairs_ref, cosine_ref, sine_ref, out):
        keys = pairs_ref[:, :share // 2].reshape(head, tokens).astype(F32)
        values = pairs_ref[:, share // 2:].reshape(head, tokens)
        keys = turn(keys, cosine_ref[...], sine_ref[...]).astype(BF16)
        scores = contract(q_ref[...], keys, 0, 0) * head ** (-0.5)
        at = lax.broadcasted_iota(jnp.int32, (tokens, tokens), 0)
        key_at = lax.broadcasted_iota(jnp.int32, (tokens, tokens), 1)
        scores = jnp.where(at >= key_at, scores, -1e30)
        weights = jnp.exp(scores - jnp.max(scores, axis=1, keepdims=True))
        weights = weights / jnp.sum(weights, axis=1, keepdims=True)
        out[0] = contract(weights.astype(BF16), values, 1, 1).astype(BF16)

    outs = jax.ShapeDtypeStruct((1, tokens, head), BF16)
    return call(body, "attention", outs, [VMEM] * 4, queries, pairs, cosine, sine)


def on_device(context, out_weight, residual, gain, q_weight, kv_weight):
    tokens, head = context.shape[1:]
    width = out_weight.shape[2]
    row = lax.axis_index("b").reshape(1)
    line = lax.axis_index("y").reshape(1)
    sections = lax.axis_size("section")

    def to_row(piece, step, distance):
        route = [
            (s * ROWS + r, (s + distance) % sections * ROWS + (r ^ step))
            for s in range(sections)
            for r in range(ROWS)
        ]
        return lax.ppermute(piece, ("section", "b"), route)

    got = exchange(out_pieces(out_weight, context), ("z", "y"))
    terms = row_terms(got, residual, row)

    pieces = in_pieces(q_weight, kv_weight[0].T, jnp.stack([lax.axis_index("z"), line[0]]))
    weights = [pieces[0]]
    for k in range(1, LINE):
        weights.append(lax.ppermute(pieces[k], "y", [(y, y ^ k) for y in range(LINE)]))

    positions = jnp.arange(tokens).astype(F32)
    frequency = THETA ** (-(jnp.arange(head // 2).astype(F32) * 2.0 / head))
    angles = frequency[:, None] * positions[None, :]
    cosine, sine = jnp.cos(angles), jnp.sin(angles)

    received = [to_row(terms[k], k, 1) for k in (2, 3, 1, 0)]
    gathered = lax.all_gather(scaled_sum(received, gain.T), "b", axis=0)
    other = lax.ppermute(gathered, "z", [(0, 1), (1, 0)])
    summed = exchange(projections(weights, gathered, other, line), "y")
    queries, pairs = head_inputs(summed, cosine, sine, width)
    return attention(queries, exchange(pairs, ("b", "z")), cosine, sine)


def solution(mesh):
    sections = mesh.devices.shape[0]
    fine = Mesh(mesh.devices.reshape(sections, ROWS, PAIR, LINE), ("section", "b", "z", "y"))
    tensor = ("b", "z", "y")
    placed = (
        P("section", None, tensor),
        P("section", tensor, None),
        P("section", None, tensor),
        P("section", tensor),
        P("section", None, tensor),
        P("section", None, tensor),
    )
    return jax.shard_map(
        on_device,
        mesh=fine,
        in_specs=placed,
        out_specs=P("section", None, tensor),
        check_vma=False,
    )
```

```python
import jax
import jax.numpy as jnp
from jax import lax
from jax.experimental import pallas as pl
from jax.experimental.pallas import tpu as pltpu
from jax.sharding import Mesh, PartitionSpec as P

THETA = 500000.0
ROWS, PAIR, LINE = 4, 2, 4
COLS = PAIR * LINE
BF16, F32 = jnp.bfloat16, jnp.float32
VMEM = pl.BlockSpec(memory_space=pltpu.VMEM)
SMEM = pl.BlockSpec(memory_space=pltpu.SMEM)
STATS = 16


def contract(lhs, rhs, lhs_dim, rhs_dim):
    return lax.dot_general(
        lhs, rhs, (((lhs_dim,), (rhs_dim,)), ((), ())), preferred_element_type=F32
    )


def exchange(pieces, axis):
    return lax.all_to_all(pieces, axis, 0, 0, tiled=True)


def turn(rows, cosine, sine):
    half = rows.shape[0] // 2
    first, second = rows[:half], rows[half:]
    return jnp.concatenate(
        [first * cosine - second * sine, second * cosine + first * sine], axis=0
    )


def stats_rows(total):
    high = total.astype(BF16).astype(F32)
    index = lax.broadcasted_iota(jnp.int32, (STATS, total.shape[1]), 0)
    low = jnp.where(index == 1, total - high, 0.0)
    return jnp.where(index == 0, high, low).astype(BF16)


def call(body, name, outs, in_specs, *operands):
    return pl.pallas_call(
        body,
        in_specs=in_specs,
        out_specs=jax.tree.map(lambda _: VMEM, outs),
        out_shape=outs,
        compiler_params=pltpu.CompilerParams(vmem_limit_bytes=40 * 2**20),
        name=name,
    )(*operands)


def out_pieces(out_weight, context):
    head, width = out_weight.shape[1:]
    tokens = context.shape[1]
    part = width // (ROWS * COLS)
    block = ROWS * part

    def body(weight, own, out):
        for r in range(ROWS):
            at = pl.multiple_of((r * COLS + pl.program_id(0)) * part, part)
            out[0, :, r * part:(r + 1) * part] = weight[0, :, pl.ds(at, part)]
        out[0, :, block:] = own[0].astype(F32).T.astype(BF16)

    return pl.pallas_call(
        body,
        grid=(COLS,),
        in_specs=[VMEM, VMEM],
        out_specs=pl.BlockSpec((1, head, block + tokens), lambda a: (a, 0, 0)),
        out_shape=jax.ShapeDtypeStruct((COLS, head, block + tokens), BF16),
        compiler_params=pltpu.CompilerParams(vmem_limit_bytes=40 * 2**20),
        name="out_pieces",
    )(out_weight, context)


def in_pieces(q_weight, kv_weight, side):
    width, head = q_weight.shape[1:]
    cols = kv_weight.shape[0]
    part = width // (ROWS * COLS)
    strips = ROWS * PAIR
    block = strips * part
    rows = block + cols * block // head

    def body(side_ref, *refs):
        q_refs, kv_refs, out = refs[:strips], refs[strips:2 * strips], refs[2 * strips]
        for r in range(strips):
            out[0, r * part:(r + 1) * part] = q_refs[r][0]
            for k in range(part // head):
                at = block + (r * (part // head) + k) * cols
                out[0, at:at + cols] = kv_refs[r][:, k * head:(k + 1) * head]

    def place(r, y, side_ref):
        return r % ROWS * COLS + (side_ref[0] ^ (r // ROWS)) * LINE + (side_ref[1] ^ y)

    def q_strip(r):
        return pl.BlockSpec((1, part, head), lambda y, s: (0, place(r, y, s), 0))

    def kv_strip(r):
        return pl.BlockSpec((cols, part), lambda y, s: (0, place(r, y, s)))

    return pl.pallas_call(
        body,
        grid_spec=pltpu.PrefetchScalarGridSpec(
            num_scalar_prefetch=1,
            grid=(LINE,),
            in_specs=[q_strip(r) for r in range(strips)]
            + [kv_strip(r) for r in range(strips)],
            out_specs=pl.BlockSpec((1, rows, head), lambda y, s: (y, 0, 0)),
        ),
        out_shape=jax.ShapeDtypeStruct((LINE, rows, head), BF16),
        name="in_pieces",
    )(side, *[q_weight] * strips, *[kv_weight] * strips)


def row_terms(got, residual, row):
    head = got.shape[1]
    tokens, part = residual.shape[1:]

    def body(row_ref, got_ref, residual_ref, *outs):
        context = got_ref[:, :, ROWS * part:].reshape(COLS * head, tokens)
        for k in range(ROWS):
            at = pl.multiple_of((row_ref[0] ^ k) * part, part)
            weight = got_ref[:, :, pl.ds(at, part)].reshape(COLS * head, part)
            terms = contract(weight, context, 0, 0)
            if k == 0:
                terms = terms + residual_ref[0].astype(F32).T
            outs[k][...] = terms.astype(BF16)

    outs = [jax.ShapeDtypeStruct((part, tokens), BF16)] * ROWS
    return call(body, "row_terms", outs, [SMEM, VMEM, VMEM], row, got, residual)


def scaled_sum(pieces, gain):
    part, tokens = pieces[0].shape

    def body(*refs):
        total = refs[0][...].astype(F32)
        for k in range(1, ROWS):
            total = total + refs[k][...].astype(F32)
        out = refs[ROWS + 1]
        out[:part] = (total * refs[ROWS][...]).astype(BF16)
        out[part:] = stats_rows(jnp.sum(total * total, axis=0, keepdims=True))

    outs = jax.ShapeDtypeStruct((part + STATS, tokens), BF16)
    return call(body, "scaled_sum", outs, [VMEM] * (ROWS + 1), *pieces, gain)


def projections(got, own, other, line):
    rows, head = got[0].shape
    tokens = own.shape[2]
    part = own.shape[1] - STATS
    half = ROWS * part
    block = PAIR * half
    chunks = block // head
    cols = (rows - block) // chunks
    each = cols // ROWS
    size = LINE * cols

    def body(line_ref, *refs):
        got_refs, (own_ref, other_ref, out) = refs[:LINE], refs[LINE:]
        sides = [ref[:, :part].reshape(half, tokens) for ref in (own_ref, other_ref)]
        features = jnp.concatenate(sides, axis=0)
        kv = jnp.zeros((size, tokens), F32)
        for k in range(chunks):
            at = block + k * cols
            weight = jnp.concatenate([ref[at:at + cols] for ref in got_refs], axis=0)
            kv = kv + contract(weight, features[k * head:(k + 1) * head], 1, 0)
        to = lax.broadcasted_iota(jnp.int32, (size, size), 0)
        source = lax.broadcasted_iota(jnp.int32, (size, size), 1)
        group, rest = to // (LINE * each), to % (LINE * each)
        kind, rest = rest // (LINE * each // 2), rest % (LINE * each // 2)
        column, feature = rest // (each // 2), rest % (each // 2)
        wanted = (column ^ line_ref[0]) * cols + group * each + kind * (each // 2) + feature
        select = jnp.where(source == wanted, 1.0, 0.0).astype(BF16)
        kv = contract(select, kv.astype(BF16), 1, 0).astype(BF16)
        squares = own_ref[:, part:].astype(F32) + other_ref[:, part:].astype(F32)
        squares = jnp.sum(jnp.sum(squares, axis=0), axis=0, keepdims=True)
        stats = stats_rows(squares)
        for y in range(LINE):
            out[line_ref[0] ^ y, :head] = contract(got_refs[y][:block], features, 0, 0).astype(BF16)
            out[y, head:head + size] = kv
            out[y, head + size:] = stats

    outs = jax.ShapeDtypeStruct((LINE, head + size + STATS, tokens), BF16)
    specs = [SMEM] + [VMEM] * (LINE + 2)
    return call(body, "projections", outs, specs, line, *got, own, other)


def head_inputs(got, cosine, sine, width):
    line, rows, tokens = got.shape
    head = 2 * cosine.shape[0]
    share = (rows - head - STATS) // ROWS

    def body(got_ref, cosine_ref, sine_ref, q_ref, kv_ref):
        total = got_ref[0].astype(F32)
        for y in range(1, line):
            total = total + got_ref[y].astype(F32)
        squares = jnp.sum(total[rows - STATS:], axis=0, keepdims=True)
        total = total[:rows - STATS] * lax.rsqrt(squares / width + 1e-05)
        q_ref[...] = turn(total[:head], cosine_ref[...], sine_ref[...]).astype(BF16)
        for r in range(ROWS):
            at = head + r * share
            for z in range(PAIR):
                kv_ref[r * PAIR + z] = total[at:at + share].astype(BF16)

    outs = [
        jax.ShapeDtypeStruct((head, tokens), BF16),
        jax.ShapeDtypeStruct((ROWS * PAIR, share, tokens), BF16),
    ]
    return call(body, "head_inputs", outs, [VMEM] * 3, got, cosine, sine)


def attention(queries, pairs, cosine, sine):
    head, tokens = queries.shape
    groups, share = pairs.shape[:2]

    def body(q_ref, pairs_ref, cosine_ref, sine_ref, out):
        keys = pairs_ref[:, :share // 2].reshape(head, tokens).astype(F32)
        values = pairs_ref[:, share // 2:].reshape(head, tokens)
        keys = turn(keys, cosine_ref[...], sine_ref[...]).astype(BF16)
        scores = contract(q_ref[...], keys, 0, 0) * head ** (-0.5)
        at = lax.broadcasted_iota(jnp.int32, (tokens, tokens), 0)
        key_at = lax.broadcasted_iota(jnp.int32, (tokens, tokens), 1)
        scores = jnp.where(at >= key_at, scores, -1e30)
        weights = jnp.exp(scores - jnp.max(scores, axis=1, keepdims=True))
        weights = weights / jnp.sum(weights, axis=1, keepdims=True)
        out[0] = contract(weights.astype(BF16), values, 1, 1).astype(BF16)

    outs = jax.ShapeDtypeStruct((1, tokens, head), BF16)
    return call(body, "attention", outs, [VMEM] * 4, queries, pairs, cosine, sine)


def on_device(context, out_weight, residual, gain, q_weight, kv_weight):
    tokens, head = context.shape[1:]
    width = out_weight.shape[2]
    row = lax.axis_index("b").reshape(1)
    line = lax.axis_index("y").reshape(1)
    sections = lax.axis_size("section")

    def to_row(piece, step, distance):
        route = [
            (s * ROWS + r, (s + distance) % sections * ROWS + (r ^ step))
            for s in range(sections)
            for r in range(ROWS)
        ]
        return lax.ppermute(piece, ("section", "b"), route)

    got = exchange(out_pieces(out_weight, context), ("z", "y"))
    terms = row_terms(got, residual, row)

    pieces = in_pieces(q_weight, kv_weight[0].T, jnp.stack([lax.axis_index("z"), line[0]]))
    weights = [pieces[0]]
    for k in range(1, LINE):
        weights.append(lax.ppermute(pieces[k], "y", [(y, y ^ k) for y in range(LINE)]))

    positions = jnp.arange(tokens).astype(F32)
    frequency = THETA ** (-(jnp.arange(head // 2).astype(F32) * 2.0 / head))
    angles = frequency[:, None] * positions[None, :]
    cosine, sine = jnp.cos(angles), jnp.sin(angles)

    received = [to_row(terms[k], k, 1) for k in (2, 3, 0, 1)]
    gathered = lax.all_gather(scaled_sum(received, gain.T), "b", axis=0)
    other = lax.ppermute(gathered, "z", [(0, 1), (1, 0)])
    summed = exchange(projections(weights, gathered, other, line), "y")
    queries, pairs = head_inputs(summed, cosine, sine, width)
    return attention(queries, exchange(pairs, ("b", "z")), cosine, sine)


def solution(mesh):
    sections = mesh.devices.shape[0]
    fine = Mesh(mesh.devices.reshape(sections, ROWS, PAIR, LINE), ("section", "b", "z", "y"))
    tensor = ("b", "z", "y")
    placed = (
        P("section", None, tensor),
        P("section", tensor, None),
        P("section", None, tensor),
        P("section", tensor),
        P("section", None, tensor),
        P("section", None, tensor),
    )
    return jax.shard_map(
        on_device,
        mesh=fine,
        in_specs=placed,
        out_specs=P("section", None, tensor),
        check_vma=False,
    )
```
